512 devices in a mesh: row: 16 (over y, core), col: 32 (over x, z).
Axes of the slice: x: 4, y: 8, z: 8, core: 2. Of those that a mesh axis runs over, the one named last changes fastest.
Arguments:
- demand: bfloat16 [196608, 128], P(('row', 'col')), may hold values from -6 to 6
- tile_data: bfloat16 [16, 32, 128, 128, 128], P('row', 'col'), may hold values from -0.078125 to 0.078125
- tile_row: int32 [16, 32, 128], P('row', 'col'), may hold values from 0 to 48, as said below
- tile_col: int32 [16, 32, 128], P('row', 'col'), may hold values from 0 to 95, as said below
Outputs:
- leontief: bfloat16 [196608, 128], P(('row', 'col'))
The draws below stay inside these ranges and needn't reach their ends.
Inputs may be any that keep to these rules, and one draw needn't show every extreme that they name: `tile_row`: the value 16 * 3 marks an empty slot. In every index pair the live slots come first and number at least 42; in every draw some index pair has all 128 slots live. Two slots may name the same tile position; their tiles then add. `tile_col`: empty slots carry a column too, which is ignored.
All inputs are finite; a program needn't handle non-finite values.
Results may differ from the reference program's by a relative error of at most 0.018.
Values may be sent and summed in bfloat16 or wider, within the bound.
No kernel may reach another device: no remote copies, remote signals or barrier semaphores. Data moves between devices by JAX's collectives and lax.ppermute only.
A program may use at most 64 MiB of HBM per device.

```python
import jax
import jax.numpy as jnp
from jax import lax

TILE = 128
SPAN = 3
COLS = 128
SLOTS = 128
SECTORS = 196608
N_ROW = 16
N_COL = 32


def draw_tile_row(key, part):
    key_count = jax.random.fold_in(key, 11)
    key_full = jax.random.fold_in(key, 12)
    key_rows = jax.random.fold_in(key, 13)
    counts = jax.random.randint(key_count, (N_ROW, N_COL), SLOTS // 3, SLOTS + 1)
    chosen = jax.random.randint(key_full, (), 0, N_ROW * N_COL)
    flat_index = jnp.arange(N_ROW * N_COL, dtype=jnp.int32).reshape(N_ROW, N_COL)
    counts = jnp.where(flat_index == chosen, SLOTS, counts)
    rows_drawn = jax.random.randint(key_rows, (N_ROW, N_COL, SLOTS), 0, N_ROW * SPAN)
    slot_index = jnp.arange(SLOTS, dtype=jnp.int32)
    live = slot_index[None, None, :] < counts[:, :, None]
    return jnp.where(live, rows_drawn, N_ROW * SPAN).astype(jnp.int32)


def draw_tile_col(key, part):
    key_cols = jax.random.fold_in(key, 21)
    return jax.random.randint(key_cols, (N_ROW, N_COL, SLOTS), 0, N_COL * SPAN).astype(jnp.int32)


def block_levels(stream_key, dims, pieces, least, largest):
    def one(position, blocks):
        steps = jax.random.uniform(jax.random.fold_in(jax.random.fold_in(stream_key, 6), position), (blocks,), jnp.float32, least / len(pieces), largest / len(pieces))
        return jnp.repeat(jnp.exp(steps), dims[position] // blocks).reshape((-1,) + (1,) * (len(dims) - position - 1))

    gain = one(*pieces[0])
    for cut in pieces[1:]:
        gain = gain * one(*cut)
    return gain


def noise(key, dims, deviation, bound, split=(), kind=jnp.bfloat16):
    drawn = deviation * jax.random.normal(key, dims, jnp.float32)
    if split:
        drawn = drawn * block_levels(key, dims, split, -0.22, 0.18)
    return jnp.clip(drawn, -bound, bound).astype(kind)


def setup_inputs(seed: int = 0) -> dict:
    key_of = jax.random.split(jax.random.key(seed), 5)
    demand = noise(key_of[0], (SECTORS, COLS), 1.0, 6.0, ((0, 512),))
    tile_data = noise(key_of[1], (N_ROW, N_COL, SLOTS, TILE, TILE), (SLOTS * TILE // SPAN) ** -0.5, 0.078125, ((0, 16), (1, 32)))
    tile_row = draw_tile_row(jax.random.fold_in(key_of[4], 71), 0)
    tile_col = draw_tile_col(jax.random.fold_in(key_of[4], 71), 0)
    return {"demand": demand, "tile_data": tile_data, "tile_row": tile_row, "tile_col": tile_col}


def multiply(panel, tile_data, tile_row, tile_col):
    columns = panel.shape[1]
    local_rows = N_ROW * SPAN
    blocks = panel.reshape(N_ROW, N_COL * SPAN, TILE, columns)
    targets = jnp.arange(local_rows, dtype=jnp.int32)

    def per_target(target):
        def accumulate(running, source):
            picked = jnp.take(blocks[source], tile_col[source, target], axis=0)
            products = jnp.einsum("stk,skc->stc", tile_data[source, target].astype(jnp.float32), picked.astype(jnp.float32))
            onehot = (tile_row[source, target][None, :] == targets[:, None]).astype(jnp.float32)
            partial_value = jnp.dot(onehot, products.reshape(SLOTS, -1), precision=lax.Precision.HIGHEST)
            partial_value = lax.optimization_barrier(partial_value.astype(jnp.bfloat16)).astype(jnp.float32)
            return running + partial_value, None

        running, _ = lax.scan(accumulate, jnp.zeros((local_rows, TILE * columns), jnp.float32), jnp.arange(N_ROW, dtype=jnp.int32))
        return running.astype(jnp.bfloat16).reshape(N_ROW, SPAN * TILE, columns)

    stacked = lax.map(per_target, jnp.arange(N_COL, dtype=jnp.int32))
    return stacked.transpose(1, 0, 2, 3).reshape(-1, columns)


def reference(demand, tile_data, tile_row, tile_col):
    first_term = multiply(demand, tile_data, tile_row, tile_col)
    second_term = multiply(first_term, tile_data, tile_row, tile_col)
    summed = demand.astype(jnp.float32) + first_term.astype(jnp.float32) + second_term.astype(jnp.float32)
    return summed.astype(jnp.bfloat16)
```

```python
import jax
import jax.numpy as jnp
from jax import lax
from jax.experimental import pallas as pl
from jax.experimental.pallas import tpu as pltpu
from jax.sharding import Mesh
from jax.sharding import PartitionSpec as P

COL = ("x", "z")
ROW_COL = ("y", "core", "x", "z")
CHUNK = 16


def spread(piece, axis):
    copies = jnp.broadcast_to(piece[None], (lax.axis_size(axis), *piece.shape))
    return lax.all_to_all(copies, axis, split_axis=0, concat_axis=0, tiled=True)


def gather_panel(piece):
    along_z = spread(piece, "z").reshape(-1, piece.shape[1])
    return spread(along_z, "x").reshape(-1, piece.shape[1])


def tile_kernel(spans, core_ref, rows_ref, cols_ref, tiles_ref, panel_ref, keep_ref, send_ref, total_ref):
    step = pl.program_id(0)
    edge = tiles_ref.shape[-1]
    span_tiles = keep_ref.shape[0] // (spans // 2 * edge)
    half = spans // 2 * span_tiles
    core = core_ref[0]

    @pl.when(step == 0)
    def _():
        total_ref[...] = jnp.zeros_like(total_ref)

    products = []
    places = []
    for slot in range(tiles_ref.shape[0]):
        col = cols_ref[step * tiles_ref.shape[0] + slot]
        block = panel_ref[pl.ds(pl.multiple_of(col * edge, edge), edge), :]
        products.append(jnp.dot(tiles_ref[slot], block, preferred_element_type=jnp.float32))
        row = rows_ref[step * tiles_ref.shape[0] + slot]
        span = row // span_tiles
        place = (span // 2) * span_tiles + row % span_tiles + half * lax.bitwise_xor(span % 2, core)
        places.append(jnp.where(row >= 2 * half, 2 * half, place))
    for product, place in zip(products, places):
        at = pl.ds(pl.multiple_of(place * edge, edge), edge)
        total_ref[at, :] += product

    @pl.when(step == pl.num_programs(0) - 1)
    def _():
        keep_ref[...] = total_ref[: half * edge].astype(keep_ref.dtype)
        send_ref[...] = total_ref[half * edge : 2 * half * edge].astype(send_ref.dtype)


def tile_products(panel, tile_block, slot_rows, slot_cols, core, spans, span_rows):
    slots, edge = tile_block.shape[0], tile_block.shape[-1]
    columns = panel.shape[1]
    half_rows = spans // 2 * span_rows
    chunk = min(CHUNK, slots)
    whole = pl.BlockSpec((half_rows, columns), lambda i, *_: (0, 0))
    return pl.pallas_call(
        lambda *refs: tile_kernel(spans, *refs),
        out_shape=[
            jax.ShapeDtypeStruct((half_rows, columns), jnp.float32),
            jax.ShapeDtypeStruct((half_rows, columns), jnp.bfloat16),
        ],
        grid_spec=pltpu.PrefetchScalarGridSpec(
            num_scalar_prefetch=3,
            grid=(slots // chunk,),
            in_specs=[
                pl.BlockSpec((chunk, edge, edge), lambda i, *_: (i, 0, 0)),
                pl.BlockSpec(panel.shape, lambda i, *_: (0, 0), pipeline_mode=pl.Buffered(1)),
            ],
            out_specs=[whole, whole],
            scratch_shapes=[pltpu.VMEM((2 * half_rows + edge, columns), jnp.float32)],
        ),
        compiler_params=pltpu.CompilerParams(
            dimension_semantics=("arbitrary",), vmem_limit_bytes=24 << 20
        ),
        cost_estimate=pl.CostEstimate(
            flops=2 * slots * edge * edge * columns,
            bytes_accessed=2 * slots * edge * edge + 2 * panel.size + 6 * half_rows * columns,
            transcendentals=0,
        ),
    )(core, slot_rows, slot_cols, tile_block, panel)


def multiply(piece, tile_block, slot_rows, slot_cols, core):
    columns = piece.shape[1]
    chips = lax.axis_size("y")
    panel = gather_panel(piece)
    keep, send = tile_products(
        panel, tile_block, slot_rows, slot_cols, core, 2 * chips, piece.shape[0]
    )
    other = lax.ppermute(send, "core", [(0, 1), (1, 0)])
    both = (keep + other.astype(jnp.float32)).astype(jnp.bfloat16)
    arrived = lax.all_to_all(
        both.reshape(chips, -1, columns), "y", split_axis=0, concat_axis=0, tiled=True
    )
    return arrived.astype(jnp.float32).sum(axis=0).astype(jnp.bfloat16)


def body(demand, tile_data, tile_row, tile_col):
    tile_block = tile_data[0, 0]
    slot_rows = tile_row[0, 0]
    slot_cols = tile_col[0, 0]
    core = lax.axis_index("core").astype(jnp.int32).reshape(1)
    first_term = multiply(demand, tile_block, slot_rows, slot_cols, core)
    second_term = multiply(first_term, tile_block, slot_rows, slot_cols, core)
    summed = (
        demand.astype(jnp.float32)
        + first_term.astype(jnp.float32)
        + second_term.astype(jnp.float32)
    )
    return summed.astype(jnp.bfloat16)


def solution(mesh):
    rows, cols = mesh.shape["row"], mesh.shape["col"]
    torus = Mesh(
        mesh.devices.reshape(rows // 2, 2, 4, cols // 4), ("y", "core", "x", "z")
    )
    return jax.shard_map(
        body,
        mesh=torus,
        in_specs=(
            P(ROW_COL, None),
            P(("y", "core"), COL, None, None, None),
            P(("y", "core"), COL, None),
            P(("y", "core"), COL, None),
        ),
        out_specs=P(ROW_COL, None),
        check_vma=False,
    )
```

```python
import jax
import jax.numpy as jnp
from jax import lax
from jax.experimental import pallas as pl
from jax.experimental.pallas import tpu as pltpu
from jax.sharding import Mesh
from jax.sharding import PartitionSpec as P

COL = ("x", "z")
ROW_COL = ("y", "core", "x", "z")
CHUNK = 16
EARLY = 96


def spread(piece, axis):
    copies = jnp.broadcast_to(piece[None], (lax.axis_size(axis), *piece.shape))
    return lax.all_to_all(copies, axis, split_axis=0, concat_axis=0, tiled=True)


def tile_kernel(slots_ref, tiles_hbm_ref, early_ref, late_ref, keep_ref, send_ref, tiles_ref, total_ref, sems):
    edge = tiles_ref.shape[-1]
    half = keep_ref.shape[0]

    def fetch(step):
        at = pl.ds(step * CHUNK, CHUNK)
        return pltpu.make_async_copy(tiles_hbm_ref.at[at], tiles_ref.at[at], sems.at[step])

    for step in range(sems.shape[0]):
        fetch(step).start()
    total_ref[...] = jnp.zeros_like(total_ref)

    @pl.loop(0, tiles_ref.shape[0] // CHUNK)
    def _(step):
        fetch(step).wait()
        products = []
        for k in range(CHUNK):
            slot = step * CHUNK + k
            is_early = slots_ref[1, slot] != 0
            early = early_ref[slots_ref[2, slot]]
            upper = late_ref[pl.ds(pl.multiple_of(slots_ref[3, slot], 32), EARLY), :]
            lower = late_ref[pl.ds(pl.multiple_of(slots_ref[4, slot], 32), edge - EARLY), :]
            block = jnp.concatenate([jnp.where(is_early, early, upper), lower], axis=0)
            products.append(jnp.dot(tiles_ref[slot], block, preferred_element_type=jnp.float32))
        for k, product in enumerate(products):
            total_ref[slots_ref[0, step * CHUNK + k]] += product

    keep_ref[...] = total_ref[:half].astype(keep_ref.dtype)
    send_ref[...] = total_ref[half : 2 * half].astype(send_ref.dtype)


def tile_products(slots, tiles, early, late, half):
    edge, columns = tiles.shape[-1], late.shape[-1]
    vmem = pl.BlockSpec(memory_space=pltpu.VMEM)
    return pl.pallas_call(
        tile_kernel,
        out_shape=[
            jax.ShapeDtypeStruct((half, edge, columns), jnp.float32),
            jax.ShapeDtypeStruct((half, edge, columns), jnp.bfloat16),
        ],
        in_specs=[pl.BlockSpec(memory_space=pltpu.SMEM), pl.BlockSpec(memory_space=pl.ANY), vmem, vmem],
        out_specs=[vmem, vmem],
        scratch_shapes=[
            pltpu.VMEM(tiles.shape, tiles.dtype),
            pltpu.VMEM((2 * half + 1, edge, columns), jnp.float32),
            pltpu.SemaphoreType.DMA((tiles.shape[0] // CHUNK,)),
        ],
        compiler_params=pltpu.CompilerParams(vmem_limit_bytes=24 << 20),
        cost_estimate=pl.CostEstimate(
            flops=2 * tiles.size * columns,
            bytes_accessed=2 * (tiles.size + early.size + late.size) + 6 * half * edge * columns,
            transcendentals=0,
        ),
    )(slots, pltpu.with_memory_space_constraint(tiles, pltpu.HBM), early.reshape(-1, EARLY, columns), late.reshape(-1, columns))


def body(demand, tile_data, tile_row, tile_col):
    tile_block = tile_data[0, 0]
    slot_rows = tile_row[0, 0]
    slot_cols = tile_col[0, 0]
    edge, columns = tile_block.shape[-1], demand.shape[1]
    chips, ring, line = lax.axis_size("y"), lax.axis_size("x"), lax.axis_size("z")
    span_tiles = demand.shape[0] // edge
    half = chips * span_tiles

    span = slot_rows // span_tiles
    other_core = lax.bitwise_xor(span % 2, lax.axis_index("core"))
    places = (span // 2) * span_tiles + slot_rows % span_tiles + half * other_core
    places = jnp.where(slot_rows >= 2 * half, 2 * half, places).astype(jnp.int32)

    device, tile = slot_cols // span_tiles, slot_cols % span_tiles
    late_rows = demand.shape[0] - EARLY
    lower_at = device * late_rows + tile * edge
    upper_at = jnp.where(tile == 0, lower_at, lower_at - EARLY)
    early_at = device % line * ring + device // line
    slots = jnp.stack([places, tile == 0, early_at, upper_at, lower_at]).astype(jnp.int32)

    def multiply(piece):
        early, late = piece[:EARLY], piece[EARLY:]
        late_line = spread(late, "z")
        early_line = lax.all_gather(early, "x")
        late_line, early_line = lax.optimization_barrier((late_line, early_line))
        late_panel = spread(late_line, "x")
        early_panel = lax.all_gather(early_line, "z")
        keep, send = tile_products(slots, tile_block, early_panel, late_panel, half)
        other = lax.ppermute(send, "core", [(0, 1), (1, 0)])
        both = (keep + other.astype(jnp.float32)).astype(jnp.bfloat16)
        arrived = lax.all_to_all(
            both.reshape(chips, -1, columns), "y", split_axis=0, concat_axis=0, tiled=True
        )
        return arrived.astype(jnp.float32).sum(axis=0).astype(jnp.bfloat16)

    first_term = multiply(demand)
    second_term = multiply(first_term)
    summed = (
        demand.astype(jnp.float32)
        + first_term.astype(jnp.float32)
        + second_term.astype(jnp.float32)
    )
    return summed.astype(jnp.bfloat16)


def solution(mesh):
    rows, cols = mesh.shape["row"], mesh.shape["col"]
    torus = Mesh(
        mesh.devices.reshape(rows // 2, 2, 4, cols // 4), ("y", "core", "x", "z")
    )
    return jax.shard_map(
        body,
        mesh=torus,
        in_specs=(
            P(ROW_COL, None),
            P(("y", "core"), COL, None, None, None),
            P(("y", "core"), COL, None),
            P(("y", "core"), COL, None),
        ),
        out_specs=P(ROW_COL, None),
        check_vma=False,
    )
```

```python
import jax
import jax.numpy as jnp
from jax import lax
from jax.experimental import pallas as pl
from jax.experimental.pallas import tpu as pltpu
from jax.sharding import Mesh
from jax.sharding import PartitionSpec as P

Z = ("z_pair", "z_end")
COL = ("x", *Z)
ROW_COL = ("y", "core", *COL)
CHUNK = 16
EARLY = 112


def spread(piece, axis):
    copies = jnp.broadcast_to(piece[None], (lax.axis_size(axis), *piece.shape))
    return lax.all_to_all(copies, axis, split_axis=0, concat_axis=0, tiled=True)


def tile_kernel(slots_ref, tiles_hbm_ref, early_ref, late_ref, keep_ref, send_ref, tiles_ref, total_ref, sems):
    edge = tiles_ref.shape[-1]
    half = keep_ref.shape[0]

    def fetch(step):
        at = pl.ds(step * CHUNK, CHUNK)
        return pltpu.make_async_copy(tiles_hbm_ref.at[at], tiles_ref.at[at], sems.at[step])

    for step in range(sems.shape[0]):
        fetch(step).start()
    total_ref[...] = jnp.zeros_like(total_ref)

    @pl.loop(0, tiles_ref.shape[0] // CHUNK)
    def _(step):
        fetch(step).wait()
        products = []
        for k in range(CHUNK):
            slot = step * CHUNK + k
            is_early = slots_ref[1, slot] != 0
            early = early_ref[slots_ref[2, slot]]
            upper = late_ref[pl.ds(pl.multiple_of(slots_ref[3, slot], 16), EARLY), :]
            lower = late_ref[pl.ds(pl.multiple_of(slots_ref[4, slot], 16), edge - EARLY), :]
            block = jnp.concatenate([jnp.where(is_early, early, upper), lower], axis=0)
            products.append(jnp.dot(tiles_ref[slot], block, preferred_element_type=jnp.float32))
        for k, product in enumerate(products):
            total_ref[slots_ref[0, step * CHUNK + k]] += product

    keep_ref[...] = total_ref[:half].astype(keep_ref.dtype)
    send_ref[...] = total_ref[half : 2 * half].astype(send_ref.dtype)


def tile_products(slots, tiles, early, late, half):
    edge, columns = tiles.shape[-1], late.shape[-1]
    vmem = pl.BlockSpec(memory_space=pltpu.VMEM)
    return pl.pallas_call(
        tile_kernel,
        out_shape=[
            jax.ShapeDtypeStruct((half, edge, columns), jnp.float32),
            jax.ShapeDtypeStruct((half, edge, columns), jnp.bfloat16),
        ],
        in_specs=[pl.BlockSpec(memory_space=pltpu.SMEM), pl.BlockSpec(memory_space=pl.ANY), vmem, vmem],
        out_specs=[vmem, vmem],
        scratch_shapes=[
            pltpu.VMEM(tiles.shape, tiles.dtype),
            pltpu.VMEM((2 * half + 1, edge, columns), jnp.float32),
            pltpu.SemaphoreType.DMA((tiles.shape[0] // CHUNK,)),
        ],
        compiler_params=pltpu.CompilerParams(vmem_limit_bytes=24 << 20),
        cost_estimate=pl.CostEstimate(
            flops=2 * tiles.size * columns,
            bytes_accessed=2 * (tiles.size + early.size + late.size) + 6 * half * edge * columns,
            transcendentals=0,
        ),
    )(slots, pltpu.with_memory_space_constraint(tiles, pltpu.HBM), early.reshape(-1, EARLY, columns), late.reshape(-1, columns))


def body(demand, tile_data, tile_row, tile_col):
    tile_block = tile_data[0, 0]
    slot_rows = tile_row[0, 0]
    slot_cols = tile_col[0, 0]
    edge, columns = tile_block.shape[-1], demand.shape[1]
    chips, ring, line = lax.axis_size("y"), lax.axis_size("x"), lax.axis_size(Z)
    span_tiles = demand.shape[0] // edge
    half = chips * span_tiles

    span = slot_rows // span_tiles
    other_core = lax.bitwise_xor(span % 2, lax.axis_index("core"))
    places = (span // 2) * span_tiles + slot_rows % span_tiles + half * other_core
    places = jnp.where(slot_rows >= 2 * half, 2 * half, places).astype(jnp.int32)

    device, tile = slot_cols // span_tiles, slot_cols % span_tiles
    late_rows = demand.shape[0] - EARLY
    lower_at = device * late_rows + tile * edge
    upper_at = jnp.where(tile == 0, lower_at, lower_at - EARLY)
    early_at = device % line * ring + device // line
    slots = jnp.stack([places, tile == 0, early_at, upper_at, lower_at]).astype(jnp.int32)

    def multiply(piece):
        early, late = piece[:EARLY], piece[EARLY:]
        late_line = spread(late, Z)
        early_line = lax.all_gather(early, "x")
        late_line, early_line = lax.optimization_barrier((late_line, early_line))
        late_panel = spread(late_line, "x")
        early_panel = lax.all_gather(lax.all_gather(early_line, "z_end"), "z_pair")
        keep, send = tile_products(slots, tile_block, early_panel, late_panel, half)
        other = lax.ppermute(send, "core", [(0, 1), (1, 0)])
        both = (keep + other.astype(jnp.float32)).astype(jnp.bfloat16)
        arrived = lax.all_to_all(
            both.reshape(chips, -1, columns), "y", split_axis=0, concat_axis=0, tiled=True
        )
        return arrived.astype(jnp.float32).sum(axis=0).astype(jnp.bfloat16)

    first_term = multiply(demand)
    second_term = multiply(first_term)
    summed = (
        demand.astype(jnp.float32)
        + first_term.astype(jnp.float32)
        + second_term.astype(jnp.float32)
    )
    return summed.astype(jnp.bfloat16)


def solution(mesh):
    rows, cols = mesh.shape["row"], mesh.shape["col"]
    torus = Mesh(
        mesh.devices.reshape(rows // 2, 2, 4, cols // 8, 2), ROW_COL
    )
    return jax.shard_map(
        body,
        mesh=torus,
        in_specs=(
            P(ROW_COL, None),
            P(("y", "core"), COL, None, None, None),
            P(("y", "core"), COL, None),
            P(("y", "core"), COL, None),
        ),
        out_specs=P(ROW_COL, None),
        check_vma=False,
    )
```

```python
import jax
import jax.numpy as jnp
from jax import lax
from jax.experimental import pallas as pl
from jax.experimental.pallas import tpu as pltpu
from jax.sharding import Mesh
from jax.sharding import PartitionSpec as P

Z = ("z_pair", "z_end")
COL = ("x", *Z)
ROW_COL = ("y", "core", *COL)
CHUNK = 16
EARLY = 112


def spread(piece, axis):
    copies = jnp.broadcast_to(piece[None], (lax.axis_size(axis), *piece.shape))
    return lax.all_to_all(copies, axis, split_axis=0, concat_axis=0, tiled=True)


def tile_kernel(slots_ref, tiles_hbm_ref, row_ref, early_ref, late_ref, keep_ref, send_ref, tiles_ref, total_ref, sems):
    edge = tiles_ref.shape[-1]
    half = keep_ref.shape[0]

    def fetch(step):
        at = pl.ds(step * CHUNK, CHUNK)
        return pltpu.make_async_copy(tiles_hbm_ref.at[at], tiles_ref.at[at], sems.at[step])

    def rows(ref, start, size):
        return ref[pl.ds(pl.multiple_of(start, 16), size), :]

    for step in range(sems.shape[0]):
        fetch(step).start()
    total_ref[...] = jnp.zeros_like(total_ref)

    @pl.loop(0, tiles_ref.shape[0] // CHUNK)
    def _(step):
        fetch(step).wait()
        products = []
        for k in range(CHUNK):
            slot = step * CHUNK + k
            early = early_ref[slots_ref[3, slot]]
            upper = rows(late_ref, slots_ref[4, slot], EARLY)
            lower = rows(late_ref, slots_ref[5, slot], edge - EARLY)
            block = jnp.concatenate([jnp.where(slots_ref[2, slot] != 0, early, upper), lower], axis=0)
            block = jnp.where(slots_ref[1, slot] != 0, rows(row_ref, slots_ref[6, slot], edge), block)
            products.append(jnp.dot(tiles_ref[slot], block, preferred_element_type=jnp.float32))
        for k, product in enumerate(products):
            total_ref[slots_ref[0, step * CHUNK + k]] += product

    keep_ref[...] = total_ref[:half].astype(keep_ref.dtype)
    send_ref[...] = total_ref[half : 2 * half].astype(send_ref.dtype)


def tile_products(slots, tiles, row, early, late, half):
    edge, columns = tiles.shape[-1], late.shape[-1]
    vmem = pl.BlockSpec(memory_space=pltpu.VMEM)
    return pl.pallas_call(
        tile_kernel,
        out_shape=[
            jax.ShapeDtypeStruct((half, edge, columns), jnp.float32),
            jax.ShapeDtypeStruct((half, edge, columns), jnp.bfloat16),
        ],
        in_specs=[pl.BlockSpec(memory_space=pltpu.SMEM), pl.BlockSpec(memory_space=pl.ANY), vmem, vmem, vmem],
        out_specs=[vmem, vmem],
        scratch_shapes=[
            pltpu.VMEM(tiles.shape, tiles.dtype),
            pltpu.VMEM((2 * half + 1, edge, columns), jnp.float32),
            pltpu.SemaphoreType.DMA((tiles.shape[0] // CHUNK,)),
        ],
        compiler_params=pltpu.CompilerParams(vmem_limit_bytes=24 << 20),
        cost_estimate=pl.CostEstimate(
            flops=2 * tiles.size * columns,
            bytes_accessed=2 * (tiles.size + early.size + late.size) + 6 * half * edge * columns,
            transcendentals=0,
        ),
    )(slots, pltpu.with_memory_space_constraint(tiles, pltpu.HBM), row.reshape(-1, columns), early.reshape(-1, EARLY, columns), late.reshape(-1, columns))


def body(demand, tile_data, tile_row, tile_col):
    tile_block = tile_data[0, 0]
    slot_rows = tile_row[0, 0]
    slot_cols = tile_col[0, 0]
    edge, columns = tile_block.shape[-1], demand.shape[1]
    chips, ring, line = lax.axis_size("y"), lax.axis_size("x"), lax.axis_size(Z)
    span_tiles = demand.shape[0] // edge
    half = chips * span_tiles

    span = slot_rows // span_tiles
    other_core = lax.bitwise_xor(span % 2, lax.axis_index("core"))
    places = (span // 2) * span_tiles + slot_rows % span_tiles + half * other_core
    places = jnp.where(slot_rows >= 2 * half, 2 * half, places).astype(jnp.int32)

    device, tile = slot_cols // span_tiles, slot_cols % span_tiles
    at_x, at_z, my_z = device // line, device % line, lax.axis_index(Z)
    late_rows = demand.shape[0] - EARLY
    own = at_z == my_z
    sent_at = jnp.where(own, 0, jnp.where(at_z == line - 1, my_z, at_z))
    lower_at = (at_x * (line - 1) + sent_at) * late_rows + tile * edge
    upper_at = jnp.where(tile == 0, lower_at, lower_at - EARLY)
    early_at = at_z * ring + at_x
    row_at = at_x * demand.shape[0] + tile * edge
    slots = jnp.stack([places, own, tile == 0, early_at, upper_at, lower_at, row_at]).astype(jnp.int32)

    def multiply(piece):
        late_line = spread(piece[EARLY:], Z)
        row = lax.all_gather(piece, "x")
        early_pair = lax.all_gather(row[:, :EARLY], "z_end")
        late_line, early_pair = lax.optimization_barrier((late_line, early_pair))
        others = lax.dynamic_update_index_in_dim(late_line, late_line[-1], my_z, 0)[:-1]
        late_panel = spread(others, "x")
        early_panel = lax.all_gather(early_pair, "z_pair")
        keep, send = tile_products(slots, tile_block, row, early_panel, late_panel, half)
        other = lax.ppermute(send, "core", [(0, 1), (1, 0)])
        both = (keep + other.astype(jnp.float32)).astype(jnp.bfloat16)
        arrived = lax.all_to_all(
            both.reshape(chips, -1, columns), "y", split_axis=0, concat_axis=0, tiled=True
        )
        return arrived.astype(jnp.float32).sum(axis=0).astype(jnp.bfloat16)

    first_term = multiply(demand)
    second_term = multiply(first_term)
    summed = (
        demand.astype(jnp.float32)
        + first_term.astype(jnp.float32)
        + second_term.astype(jnp.float32)
    )
    return summed.astype(jnp.bfloat16)


def solution(mesh):
    rows, cols = mesh.shape["row"], mesh.shape["col"]
    torus = Mesh(
        mesh.devices.reshape(rows // 2, 2, 4, cols // 8, 2), ROW_COL
    )
    return jax.shard_map(
        body,
        mesh=torus,
        in_specs=(
            P(ROW_COL, None),
            P(("y", "core"), COL, None, None, None),
            P(("y", "core"), COL, None),
            P(("y", "core"), COL, None),
        ),
        out_specs=P(ROW_COL, None),
        check_vma=False,
    )
```

```python
import jax
import jax.numpy as jnp
from jax import lax
from jax.experimental import pallas as pl
from jax.experimental.pallas import tpu as pltpu
from jax.sharding import Mesh
from jax.sharding import PartitionSpec as P

Z = ("z_pair", "z_end")
COL = ("x", *Z)
ROW_COL = ("y", "core", *COL)
CHUNK = 32
EARLY = 112


def spread(piece, axis):
    copies = jnp.broadcast_to(piece[None], (lax.axis_size(axis), *piece.shape))
    return lax.all_to_all(copies, axis, split_axis=0, concat_axis=0, tiled=True)


def tile_kernel(slots_ref, tiles_hbm_ref, row_ref, early_ref, late_ref, total_ref, send_ref, tiles_ref, sems):
    edge = tiles_ref.shape[-1]
    half = send_ref.shape[0]

    def fetch(step):
        at = pl.ds(step * CHUNK, CHUNK)
        return pltpu.make_async_copy(tiles_hbm_ref.at[at], tiles_ref.at[at], sems.at[step])

    def rows(ref, start, size):
        return ref[pl.ds(pl.multiple_of(start, 16), size), :]

    for step in range(sems.shape[0]):
        fetch(step).start()
    total_ref[...] = jnp.zeros_like(total_ref)

    @pl.loop(0, tiles_ref.shape[0] // CHUNK)
    def _(step):
        fetch(step).wait()
        products = []
        for k in range(CHUNK):
            slot = step * CHUNK + k
            early = early_ref[slots_ref[3, slot]]
            upper = rows(late_ref, slots_ref[4, slot], EARLY)
            lower = rows(late_ref, slots_ref[5, slot], edge - EARLY)
            block = jnp.concatenate([jnp.where(slots_ref[2, slot] != 0, early, upper), lower], axis=0)
            block = jnp.where(slots_ref[1, slot] != 0, rows(row_ref, slots_ref[6, slot], edge), block)
            products.append(jnp.dot(tiles_ref[slot], block, preferred_element_type=jnp.float32))
        for k, product in enumerate(products):
            total_ref[slots_ref[0, step * CHUNK + k]] += product

    send_ref[...] = total_ref[half : 2 * half].astype(send_ref.dtype)


def tile_products(slots, tiles, row, early, late, half):
    edge, columns = tiles.shape[-1], late.shape[-1]
    vmem = pl.BlockSpec(memory_space=pltpu.VMEM)
    return pl.pallas_call(
        tile_kernel,
        out_shape=[
            jax.ShapeDtypeStruct((2 * half + 1, edge, columns), jnp.float32),
            jax.ShapeDtypeStruct((half, edge, columns), jnp.bfloat16),
        ],
        in_specs=[pl.BlockSpec(memory_space=pltpu.SMEM), pl.BlockSpec(memory_space=pl.ANY), vmem, vmem, vmem],
        out_specs=[vmem, vmem],
        scratch_shapes=[
            pltpu.VMEM(tiles.shape, tiles.dtype),
            pltpu.SemaphoreType.DMA((tiles.shape[0] // CHUNK,)),
        ],
        compiler_params=pltpu.CompilerParams(vmem_limit_bytes=24 << 20),
        cost_estimate=pl.CostEstimate(
            flops=2 * tiles.size * columns,
            bytes_accessed=2 * (tiles.size + early.size + late.size) + 6 * half * edge * columns,
            transcendentals=0,
        ),
    )(slots, pltpu.with_memory_space_constraint(tiles, pltpu.HBM), row.reshape(-1, columns), early.reshape(-1, EARLY, columns), late.reshape(-1, columns))


def body(demand, tile_data, tile_row, tile_col):
    tile_block = tile_data[0, 0]
    slot_rows = tile_row[0, 0]
    slot_cols = tile_col[0, 0]
    edge, columns = tile_block.shape[-1], demand.shape[1]
    chips, ring, line = lax.axis_size("y"), lax.axis_size("x"), lax.axis_size(Z)
    span_tiles = demand.shape[0] // edge
    half = chips * span_tiles

    span = slot_rows // span_tiles
    other_core = lax.bitwise_xor(span % 2, lax.axis_index("core"))
    places = (span // 2) * span_tiles + slot_rows % span_tiles + half * other_core
    places = jnp.where(slot_rows >= 2 * half, 2 * half, places).astype(jnp.int32)

    device, tile = slot_cols // span_tiles, slot_cols % span_tiles
    at_x, at_z, my_z = device // line, device % line, lax.axis_index(Z)
    late_rows = demand.shape[0] - EARLY
    own = at_z == my_z
    sent_at = jnp.where(own, 0, jnp.where(at_z == line - 1, my_z, at_z))
    lower_at = (at_x * (line - 1) + sent_at) * late_rows + tile * edge
    upper_at = jnp.where(tile == 0, lower_at, lower_at - EARLY)
    early_at = at_z * ring + at_x
    row_at = at_x * demand.shape[0] + tile * edge
    slots = jnp.stack([places, own, tile == 0, early_at, upper_at, lower_at, row_at]).astype(jnp.int32)

    def multiply(piece):
        late_line = spread(piece[EARLY:], Z)
        row = lax.all_gather(piece, "x")
        early_pair = lax.all_gather(row[:, :EARLY], "z_end")
        late_line, early_pair = lax.optimization_barrier((late_line, early_pair))
        others = lax.dynamic_update_index_in_dim(late_line, late_line[-1], my_z, 0)[:-1]
        late_panel = spread(others, "x")
        early_panel = lax.all_gather(early_pair, "z_pair")
        total, send = tile_products(slots, tile_block, row, early_panel, late_panel, half)
        other = lax.ppermute(send, "core", [(0, 1), (1, 0)])
        both = (total[:half] + other.astype(jnp.float32)).astype(jnp.bfloat16)
        arrived = lax.all_to_all(
            both.reshape(chips, -1, columns), "y", split_axis=0, concat_axis=0, tiled=True
        )
        return arrived.astype(jnp.float32).sum(axis=0).astype(jnp.bfloat16)

    first_term = multiply(demand)
    second_term = multiply(first_term)
    summed = (
        demand.astype(jnp.float32)
        + first_term.astype(jnp.float32)
        + second_term.astype(jnp.float32)
    )
    return summed.astype(jnp.bfloat16)


def solution(mesh):
    rows, cols = mesh.shape["row"], mesh.shape["col"]
    torus = Mesh(
        mesh.devices.reshape(rows // 2, 2, 4, cols // 8, 2), ROW_COL
    )
    return jax.shard_map(
        body,
        mesh=torus,
        in_specs=(
            P(ROW_COL, None),
            P(("y", "core"), COL, None, None, None),
            P(("y", "core"), COL, None),
            P(("y", "core"), COL, None),
        ),
        out_specs=P(ROW_COL, None),
        check_vma=False,
    )
```
